32 devices in a mesh: groups: 2 (over y), blk: 4 (over z), sub: 4 (over x, core).
Axes of the slice: x: 2, y: 2, z: 4, core: 2. Of those that a mesh axis runs over, the one named last changes fastest.
Arguments:
- strain: bfloat16 [4096, 2048], P(('groups', 'blk', 'sub')), parts along dimension 0, may hold values from -500 to 500, as said below
- fir_taps: bfloat16 [128], replicated, may hold values from -0.5 to 0.5
- live_mask: int32 [4096], P(('groups', 'blk')), parts along dimension 0, may hold values 0 or 1
- offset_band: int32 [8, 3, 2], P(('groups', 'blk')), parts along dimension 0, may hold values from -1023 to 1023, as said below
Outputs:
- noise_stack: float32 [8, 16, 2048], P(('groups', 'blk'), 'sub'), parts along dimension 0
The draws below stay inside these ranges and needn't reach their ends.
There are 2 independent parts, one for each index of `groups`. The reference program is written for one: setup_inputs(seed, part) draws one part's arguments, and reference() takes and returns one part's arrays. A program takes and returns all parts, laid end to end along the dimension named above; an argument that names none is the same for every part. Nothing has to cross between parts.
Inputs may be any that keep to these rules, and one draw needn't show every extreme that they name: `strain`: strain of every channel, of varying strength from channel to channel and over time. For pair index r (distance d = r - 1) offset_band[i, r, 0] <= offset_band[i, r, 1], both within d * 512 - 511 and d * 512 + 511.
All inputs are finite; a program needn't handle non-finite values. No bound on the sum of `live_mask` on one device may be relied on, other than what follows from the above.
Results may differ from the reference program's by a relative error of at most 0.0029.
Values may be sent and summed in bfloat16 or wider, within the bound.
A program may use at most 64 MiB of HBM per device.

```python
import math
import jax
import jax.numpy as jnp
from jax import lax

PANEL = 512
RAW = 2048
DEC = 4
TAPS = 128
LAGS = 16
PANELS = 4
CHANNELS = 2048
TIME = 512
REACH = 1
PAIRS = 3
OFFSETS = 2048


def draw_strain(key, part):
    subkeys = jax.random.split(key, 3)
    noise_field = jnp.clip(jax.random.normal(subkeys[0], (CHANNELS, RAW), jnp.float32), -4.0, 4.0)
    channel_scale = jnp.exp(jax.random.uniform(subkeys[1], (CHANNELS, 1), jnp.float32, 0.0, 2.3))
    envelope = jnp.exp(jax.random.uniform(subkeys[2], (CHANNELS, RAW // 64, 1), jnp.float32, 0.0, 2.3))
    shaped = noise_field.reshape(CHANNELS, RAW // 64, 64) * envelope
    return (shaped.reshape(CHANNELS, RAW) * channel_scale).astype(jnp.bfloat16)


def draw_offset_band(key, part):
    subkeys = jax.random.split(jax.random.fold_in(key, 17), 2)
    distance = jnp.arange(PAIRS, dtype=jnp.int32) - REACH
    centre = distance * PANEL
    lowest = centre - (PANEL - 1) + jax.random.randint(subkeys[0], (PANELS, PAIRS), 0, PANEL // 2, dtype=jnp.int32)
    highest = centre + (PANEL - 1) - jax.random.randint(subkeys[1], (PANELS, PAIRS), 0, PANEL // 2, dtype=jnp.int32)
    lowest = jnp.where(distance == -REACH, -REACH * PANEL - PANEL + 1, lowest)
    highest = jnp.where(distance == REACH, REACH * PANEL + PANEL - 1, highest)
    return jnp.stack([lowest, highest], axis=-1).astype(jnp.int32)


def place_ends(array, rng, least, largest):
    longest = array.shape.index(max(array.shape))
    spots = []
    for shift in (0, 1):
        where = [jax.random.randint(jax.random.fold_in(rng, axis), (), 0, length) for axis, length in enumerate(array.shape)]
        where[longest] = (where[longest] + shift) % array.shape[longest]
        spots.append(tuple(where))
    return array.at[spots[0]].set(least).at[spots[1]].set(largest)


def centred(stream_key, shape, deviation, reach, kind=jnp.bfloat16):
    array = deviation * jax.random.normal(stream_key, shape, jnp.float32)
    return jnp.clip(array, min=-reach, max=reach).astype(kind)


def setup_inputs(seed: int = 0, part: int = 0) -> dict:
    splits = jax.random.split(jax.random.key(seed), 5)
    part_keys = jax.random.split(jax.random.fold_in(splits[4], part), 5)
    strain = draw_strain(jax.random.fold_in(jax.random.fold_in(splits[4], part), 71), part)
    fir_taps = centred(splits[1], (TAPS,), TAPS ** -0.5, 0.5)
    live_mask = place_ends((jax.random.randint(part_keys[2], (CHANNELS,), 0, 8) < 7).astype(jnp.int32), jax.random.fold_in(part_keys[2], 1), 0, 1)
    offset_band = draw_offset_band(jax.random.fold_in(jax.random.fold_in(splits[4], part), 71), part)
    return {"strain": strain, "fir_taps": fir_taps, "live_mask": live_mask, "offset_band": offset_band}


def diagonal_totals(matrix):
    height = matrix.shape[-2]
    breadth = matrix.shape[-1]
    leading = matrix.shape[:-2]
    flipped = jnp.flip(matrix, axis=-2)
    widths = [(0, 0)] * len(leading) + [(0, 0), (0, height)]
    padded = jnp.pad(flipped, widths)
    flattened = padded.reshape(leading + (height * (breadth + height),))
    trimmed = flattened[..., :height * (breadth + height - 1)]
    skewed = trimmed.reshape(leading + (height, breadth + height - 1))
    totals = lax.optimization_barrier(jnp.sum(skewed, axis=-2))
    return jnp.pad(totals, [(0, 0)] * len(leading) + [(0, 1)])

def filter_normalize(strain, fir_taps):
    channels = strain.shape[0]
    phase_count = TAPS // DEC
    grouped = strain.astype(jnp.float32).reshape(channels, TIME, DEC)
    padded = jnp.pad(grouped, ((0, 0), (phase_count - 1, 0), (0, 0)))
    phases = fir_taps.astype(jnp.float32).reshape(phase_count, DEC)
    filtered = jnp.zeros((channels, TIME), jnp.float32)
    for quarter in range(phase_count):
        filtered = filtered + jnp.einsum('ctp,p->ct', padded[:, quarter:quarter + TIME, :], phases[quarter], precision=lax.Precision.HIGHEST)
    mean_square = lax.optimization_barrier(jnp.mean(filtered * filtered, axis=1, keepdims=True))
    return filtered / jnp.sqrt(mean_square + 1e-06)

def reference(strain, fir_taps, live_mask, offset_band):
    live_weights = live_mask.astype(jnp.float32)
    normed = (filter_normalize(strain, fir_taps) * live_weights[:, None]).astype(jnp.bfloat16)
    panels = normed.reshape(PANELS, PANEL, TIME)
    panel_live = live_weights.reshape(PANELS, PANEL)

    def one_panel(panel_index):
        resident = lax.dynamic_index_in_dim(panels, panel_index, 0, keepdims=False).astype(jnp.float32)
        own_live = lax.dynamic_index_in_dim(panel_live, panel_index, 0, keepdims=False)
        extended = jnp.pad(resident, ((0, 0), (LAGS - 1, 0)))
        lagged = jnp.stack([extended[:, LAGS - 1 - lag_step:LAGS - 1 - lag_step + TIME] for lag_step in range(LAGS)])
        stack_total = jnp.zeros((LAGS, OFFSETS), jnp.float32)
        count_total = jnp.zeros((OFFSETS,), jnp.float32)
        for distance in range(-REACH, REACH + 1):
            partner = panel_index + distance
            inside = jnp.logical_and(partner >= 0, partner < PANELS)
            clipped = jnp.clip(partner, 0, PANELS - 1).astype(jnp.int32)
            visiting = lax.dynamic_index_in_dim(panels, clipped, 0, keepdims=False).astype(jnp.float32)
            partner_live = lax.dynamic_index_in_dim(panel_live, clipped, 0, keepdims=False)
            correlation = jnp.einsum('lat,bt->lab', lagged, visiting, precision=lax.Precision.HIGHEST)
            totals = diagonal_totals(correlation)
            counts = diagonal_totals(own_live[:, None] * partner_live[None, :])
            offsets = distance * PANEL + jnp.arange(2 * PANEL, dtype=jnp.int32) - (PANEL - 1)
            lowest = offset_band[panel_index, distance + REACH, 0]
            highest = offset_band[panel_index, distance + REACH, 1]
            in_band = ((offsets >= lowest) & (offsets <= highest) & inside).astype(jnp.float32)
            column_start = (distance + REACH) * PANEL
            stack_total = stack_total.at[:, column_start:column_start + 2 * PANEL].add(totals * in_band)
            count_total = count_total.at[column_start:column_start + 2 * PANEL].add(counts * in_band)
        return stack_total / jnp.maximum(count_total, 1.0) / math.sqrt(TIME)
    return lax.map(one_panel, jnp.arange(PANELS, dtype=jnp.int32))
```

```python
import functools
import math

import jax
import jax.numpy as jnp
from jax import lax
from jax.experimental import pallas as pl
from jax.experimental.pallas import tpu as pltpu
from jax.sharding import PartitionSpec as P

PANEL = 512
DEC = 4
TAPS = 128
LAGS = 16
LANES = 128
MESH = pl.DeviceIdType.MESH


def shift_right(chunks, amount):
    lane = lax.broadcasted_iota(jnp.int32, chunks[0].shape, 1)
    rolled = [pltpu.roll(chunk, amount, 1) for chunk in chunks]
    before = [jnp.zeros_like(chunks[0])] + rolled[:-1]
    return [jnp.where(lane < amount, b, r) for b, r in zip(before, rolled)]


def diagonal_totals(matrix):
    blocks = PANEL // LANES
    chunks = []
    for j in range(1 - blocks, blocks):
        total = None
        for row in range(max(0, -j), min(blocks, blocks - j)):
            piece = matrix[
                row * LANES : (row + 1) * LANES, (row + j) * LANES : (row + j + 1) * LANES
            ]
            total = piece if total is None else total + piece
        chunks.append(total)
    chunks.append(jnp.zeros_like(chunks[0]))
    half = LANES // 2
    while half >= 8:
        low = shift_right([chunk[:half] for chunk in chunks], half)
        chunks = [a + b[half : 2 * half] for a, b in zip(low, chunks)]
        half //= 2
    row = lax.broadcasted_iota(jnp.int32, chunks[0].shape, 0)
    for bit in (4, 2, 1):
        moved = shift_right(chunks, bit)
        chunks = [jnp.where((row & bit) == 0, m, c) for m, c in zip(moved, chunks)]
    return jnp.concatenate([jnp.sum(c, axis=0, keepdims=True) for c in chunks], axis=1)


def filtered_normalized(strain_ref, taps_ref, own_live):
    channels, raw_length = strain_ref.shape
    time_length = raw_length // DEC
    span = LANES * DEC
    taps = jnp.concatenate([taps_ref[...], jnp.zeros((1, span), jnp.float32)], axis=1)
    bank = jnp.broadcast_to(taps, (LANES, span + TAPS))
    bank = pltpu.roll(bank, DEC, 1, stride=DEC, stride_axis=0).astype(jnp.bfloat16)
    pieces = []
    for block in range(time_length // LANES):
        if block == 0:
            window = jnp.concatenate(
                [jnp.zeros((channels, TAPS), jnp.bfloat16), strain_ref[:, :span]], axis=1
            )
        else:
            window = strain_ref[:, block * span - TAPS : (block + 1) * span]
        pieces.append(
            lax.dot_general(
                window, bank, (((1,), (1,)), ((), ())), preferred_element_type=jnp.float32
            )
        )
    filtered = jnp.concatenate(pieces, axis=1)
    mean_square = jnp.mean(filtered * filtered, axis=1, keepdims=True)
    return (own_live * (filtered / jnp.sqrt(mean_square + 1e-6))).astype(jnp.bfloat16)


def kernel(
    panel_count,
    sub_count,
    reach,
    strain_ref,
    taps_ref,
    live_ref,
    band_ref,
    out_ref,
    panels,
    lives,
    lagged,
    across_send,
    partner_send,
    along_send,
    live_send,
    arrival,
    live_arrival,
):
    channels = strain_ref.shape[0]
    time_length = strain_ref.shape[1] // DEC
    chip_count = sub_count // 2
    lag_count = LAGS // sub_count
    position = lax.axis_index("blk")
    me = lax.axis_index("sub")
    core = lax.rem(me, 2)
    chip = lax.div(me, 2)
    partner = chip * 2 + 1 - core
    distances = [d for step in range(1, reach + 1) for d in (-step, step)]

    def inside(d):
        return jnp.logical_and(position + d >= 0, position + d < panel_count)

    def chip_at(step):
        return lax.rem(chip + step, chip_count)

    barrier = pltpu.get_barrier_semaphore()
    pl.semaphore_signal(barrier, inc=1, device_id={"sub": partner}, device_id_type=MESH)
    for step in range(1, chip_count):
        pl.semaphore_signal(
            barrier, inc=1, device_id={"sub": chip_at(step) * 2 + core}, device_id_type=MESH
        )
    for d in distances:

        @pl.when(inside(d))
        def _():
            pl.semaphore_signal(
                barrier, inc=1, device_id={"blk": position + d}, device_id_type=MESH
            )

    row = lax.broadcasted_iota(jnp.int32, (channels, PANEL), 0)
    column = lax.broadcasted_iota(jnp.int32, (channels, PANEL), 1)
    live_row = live_ref[...].astype(jnp.float32)
    own_live = jnp.sum(
        jnp.where(column == row + me * channels, live_row, 0.0), axis=1, keepdims=True
    )
    panels[reach, me] = filtered_normalized(strain_ref, taps_ref, own_live)

    pl.semaphore_wait(
        barrier,
        chip_count
        + jnp.minimum(position, reach)
        + jnp.minimum(panel_count - 1 - position, reach),
    )

    def across(step):
        return pltpu.make_async_remote_copy(
            src_ref=panels.at[reach, me],
            dst_ref=panels.at[reach, me],
            send_sem=across_send.at[step],
            recv_sem=arrival.at[reach, me],
            device_id={"sub": chip_at(step) * 2 + core},
            device_id_type=MESH,
        )

    def to_partner(d, step):
        shard = chip_at(step) * 2 + core
        return pltpu.make_async_remote_copy(
            src_ref=panels.at[d + reach, shard],
            dst_ref=panels.at[d + reach, shard],
            send_sem=partner_send.at[d + reach, step],
            recv_sem=arrival.at[d + reach, shard],
            device_id={"sub": partner},
            device_id_type=MESH,
        )

    def along(d, step):
        shard = chip_at(step) * 2 + core
        return pltpu.make_async_remote_copy(
            src_ref=panels.at[reach, shard],
            dst_ref=panels.at[reach - d, shard],
            send_sem=along_send.at[d + reach, step],
            recv_sem=arrival.at[reach - d, shard],
            device_id={"blk": position + d},
            device_id_type=MESH,
        )

    def along_live(d):
        return pltpu.make_async_remote_copy(
            src_ref=live_ref,
            dst_ref=lives.at[reach - d],
            send_sem=live_send.at[d + reach],
            recv_sem=live_arrival.at[reach - d],
            device_id={"blk": position + d},
            device_id_type=MESH,
        )

    def arrived(d, shard):
        pltpu.make_async_copy(
            panels.at[d + reach, shard], panels.at[d + reach, shard], arrival.at[d + reach, shard]
        ).wait()

    for step in range(1, chip_count):
        across(step).start()
    for d in distances:

        @pl.when(inside(d))
        def _():
            along(d, 0).start()
            along_live(d).start()

    to_partner(0, 0).start()

    own_row = lax.broadcasted_iota(jnp.int32, (PANEL, PANEL), 0)
    own_column = lax.broadcasted_iota(jnp.int32, (PANEL, PANEL), 1)
    live_column = jnp.sum(
        jnp.where(own_row == own_column, live_row, 0.0), axis=1, keepdims=True
    )
    out_ref[...] = jnp.zeros_like(out_ref)

    for step in range(1, chip_count):
        arrived(0, chip_at(step) * 2 + core)
        to_partner(0, step).start()
        for d in distances:

            @pl.when(inside(d))
            def _():
                along(d, step).start()

    for d in distances:

        @pl.when(inside(d))
        def _():
            arrived(d, me)
            to_partner(d, 0).start()

    for step in range(chip_count):
        arrived(0, chip_at(step) * 2 + 1 - core)

    first_lag = me * lag_count
    own = panels[reach].reshape(PANEL, time_length).astype(jnp.float32)
    chunks = [own[:, i : i + LANES] for i in range(0, time_length, LANES)]
    chunks = shift_right(chunks, first_lag)
    for lag in range(lag_count):
        if lag:
            chunks = shift_right(chunks, 1)
        lagged[lag] = jnp.concatenate(chunks, axis=1).astype(jnp.bfloat16)

    def correlate(d):
        visiting = panels[d + reach].reshape(PANEL, time_length)
        rows = []
        for lag in range(lag_count):
            correlation = lax.dot_general(
                lagged[lag],
                visiting,
                (((1,), (1,)), ((), ())),
                preferred_element_type=jnp.float32,
            )
            rows.append(diagonal_totals(correlation))
        flags = live_ref[...] if d == 0 else lives[d + reach]
        rows.append(diagonal_totals(live_column * flags.astype(jnp.float32)))
        totals = jnp.concatenate(rows, axis=0)
        offset = (
            lax.broadcasted_iota(jnp.int32, totals.shape, 1) + d * PANEL - (PANEL - 1)
        )
        kept = jnp.logical_and(
            offset >= band_ref[0, d + reach, 0], offset <= band_ref[0, d + reach, 1]
        )
        kept = jnp.logical_and(kept, offset < d * PANEL + PANEL)
        start = (d + reach) * PANEL
        window = (slice(0, lag_count + 1), slice(start, start + 2 * PANEL))
        out_ref[window] += jnp.where(kept, totals, 0.0)

    correlate(0)

    for step in range(1, chip_count):
        for d in distances:

            @pl.when(inside(d))
            def _():
                arrived(d, chip_at(step) * 2 + core)
                to_partner(d, step).start()

    for d in distances:

        @pl.when(inside(d))
        def _():
            for step in range(chip_count):
                arrived(d, chip_at(step) * 2 + 1 - core)
            pltpu.make_async_copy(
                lives.at[d + reach], lives.at[d + reach], live_arrival.at[d + reach]
            ).wait()
            correlate(d)

    for step in range(1, chip_count):
        across(step).wait_send()
    for step in range(chip_count):
        to_partner(0, step).wait_send()
    for d in distances:

        @pl.when(inside(d))
        def _():
            along_live(d).wait_send()
            for step in range(chip_count):
                along(d, step).wait_send()
                to_partner(d, step).wait_send()


def on_device(strain, fir_taps, live_mask, offset_band):
    channels, raw_length = strain.shape
    time_length = raw_length // DEC
    panel_count = lax.axis_size("blk")
    sub_count = lax.axis_size("sub")
    reach = max(1, panel_count // 8)
    slots = 2 * reach + 1
    chip_count = sub_count // 2
    lag_count = LAGS // sub_count
    width = (2 * reach + 2) * PANEL
    vmem = pl.BlockSpec(memory_space=pltpu.VMEM)
    dma = pltpu.SemaphoreType.DMA
    sums = pl.pallas_call(
        functools.partial(kernel, panel_count, sub_count, reach),
        out_shape=jax.ShapeDtypeStruct((8, width), jnp.float32),
        in_specs=[vmem, vmem, vmem, pl.BlockSpec(memory_space=pltpu.SMEM)],
        out_specs=vmem,
        scratch_shapes=[
            pltpu.VMEM((slots, sub_count, channels, time_length), jnp.bfloat16),
            pltpu.VMEM((slots, 1, PANEL), jnp.int32),
            pltpu.VMEM((lag_count, PANEL, time_length), jnp.bfloat16),
            dma((chip_count,)),
            dma((slots, chip_count)),
            dma((slots, chip_count)),
            dma((slots,)),
            dma((slots, sub_count)),
            dma((slots,)),
        ],
        compiler_params=pltpu.CompilerParams(collective_id=0, has_side_effects=True),
    )(
        strain,
        fir_taps.astype(jnp.float32).reshape(1, TAPS),
        live_mask.reshape(1, PANEL),
        offset_band,
    )
    stack, count = sums[:lag_count], sums[lag_count : lag_count + 1]
    return (stack / jnp.maximum(count, 1.0) / math.sqrt(time_length))[None]


def solution(mesh):
    in_specs = (
        P(("groups", "blk", "sub"), None),
        P(),
        P(("groups", "blk")),
        P(("groups", "blk"), None, None),
    )
    out_specs = P(("groups", "blk"), "sub", None)
    return jax.shard_map(
        on_device, mesh=mesh, in_specs=in_specs, out_specs=out_specs, check_vma=False
    )
```

```python
import functools
import math

import jax
import jax.numpy as jnp
from jax import lax
from jax.experimental import pallas as pl
from jax.experimental.pallas import tpu as pltpu
from jax.sharding import PartitionSpec as P

PANEL = 512
DEC = 4
TAPS = 128
LAGS = 16
LANES = 128
MESH = pl.DeviceIdType.MESH


def shift_right(chunks, amount):
    lane = lax.broadcasted_iota(jnp.int32, chunks[0].shape, 1)
    rolled = [pltpu.roll(chunk, amount, 1) for chunk in chunks]
    before = [jnp.zeros_like(chunks[0])] + rolled[:-1]
    return [jnp.where(lane < amount, b, r) for b, r in zip(before, rolled)]


def diagonal_totals(matrix):
    blocks = PANEL // LANES
    chunks = []
    for j in range(1 - blocks, blocks):
        total = None
        for row in range(max(0, -j), min(blocks, blocks - j)):
            piece = matrix[
                row * LANES : (row + 1) * LANES, (row + j) * LANES : (row + j + 1) * LANES
            ]
            total = piece if total is None else total + piece
        chunks.append(total)
    chunks.append(jnp.zeros_like(chunks[0]))
    half = LANES // 2
    while half >= 8:
        low = shift_right([chunk[:half] for chunk in chunks], half)
        chunks = [a + b[half : 2 * half] for a, b in zip(low, chunks)]
        half //= 2
    row = lax.broadcasted_iota(jnp.int32, chunks[0].shape, 0)
    for bit in (4, 2, 1):
        moved = shift_right(chunks, bit)
        chunks = [jnp.where((row & bit) == 0, m, c) for m, c in zip(moved, chunks)]
    return jnp.concatenate([jnp.sum(c, axis=0, keepdims=True) for c in chunks], axis=1)


def filtered_normalized(strain_ref, taps_ref, own_live):
    channels, raw_length = strain_ref.shape
    time_length = raw_length // DEC
    span = LANES * DEC
    taps = jnp.concatenate([taps_ref[...].astype(jnp.float32).reshape(1, TAPS), jnp.zeros((1, span), jnp.float32)], axis=1)
    bank = jnp.broadcast_to(taps, (LANES, span + TAPS))
    bank = pltpu.roll(bank, DEC, 1, stride=DEC, stride_axis=0).astype(jnp.bfloat16)
    pieces = []
    for block in range(time_length // LANES):
        if block == 0:
            window = jnp.concatenate(
                [jnp.zeros((channels, TAPS), jnp.bfloat16), strain_ref[:, :span]], axis=1
            )
        else:
            window = strain_ref[:, block * span - TAPS : (block + 1) * span]
        pieces.append(
            lax.dot_general(
                window, bank, (((1,), (1,)), ((), ())), preferred_element_type=jnp.float32
            )
        )
    filtered = jnp.concatenate(pieces, axis=1)
    mean_square = jnp.mean(filtered * filtered, axis=1, keepdims=True)
    return (own_live * (filtered / jnp.sqrt(mean_square + 1e-6))).astype(jnp.bfloat16)


def kernel(
    panel_count,
    sub_count,
    reach,
    strain_ref,
    taps_ref,
    live_ref,
    band_ref,
    out_ref,
    panels,
    lives,
    lagged,
    sums,
    across_send,
    partner_send,
    along_send,
    live_send,
    arrival,
    live_arrival,
):
    channels = strain_ref.shape[0]
    time_length = strain_ref.shape[1] // DEC
    chip_count = sub_count // 2
    lag_count = LAGS // sub_count
    position = lax.axis_index("blk")
    me = lax.axis_index("sub")
    core = lax.rem(me, 2)
    chip = lax.div(me, 2)
    partner = chip * 2 + 1 - core
    distances = [d for step in range(1, reach + 1) for d in (-step, step)]

    def inside(d):
        return jnp.logical_and(position + d >= 0, position + d < panel_count)

    def chip_at(step):
        return lax.rem(chip + step, chip_count)

    barrier = pltpu.get_barrier_semaphore()
    pl.semaphore_signal(barrier, inc=1, device_id={"sub": partner}, device_id_type=MESH)
    for step in range(1, chip_count):
        pl.semaphore_signal(
            barrier, inc=1, device_id={"sub": chip_at(step) * 2 + core}, device_id_type=MESH
        )
    for d in distances:

        @pl.when(inside(d))
        def _():
            pl.semaphore_signal(
                barrier, inc=1, device_id={"blk": position + d}, device_id_type=MESH
            )

    row = lax.broadcasted_iota(jnp.int32, (channels, PANEL), 0)
    column = lax.broadcasted_iota(jnp.int32, (channels, PANEL), 1)
    live_row = live_ref[...].astype(jnp.float32)
    own_live = jnp.sum(
        jnp.where(column == row + me * channels, live_row, 0.0), axis=1, keepdims=True
    )
    panels[reach, me] = filtered_normalized(strain_ref, taps_ref, own_live)

    pl.semaphore_wait(
        barrier,
        chip_count
        + jnp.minimum(position, reach)
        + jnp.minimum(panel_count - 1 - position, reach),
    )

    def across(step):
        return pltpu.make_async_remote_copy(
            src_ref=panels.at[reach, me],
            dst_ref=panels.at[reach, me],
            send_sem=across_send.at[step],
            recv_sem=arrival.at[reach, me],
            device_id={"sub": chip_at(step) * 2 + core},
            device_id_type=MESH,
        )

    def to_partner(d, step):
        shard = chip_at(step) * 2 + core
        return pltpu.make_async_remote_copy(
            src_ref=panels.at[d + reach, shard],
            dst_ref=panels.at[d + reach, shard],
            send_sem=partner_send.at[d + reach, step],
            recv_sem=arrival.at[d + reach, shard],
            device_id={"sub": partner},
            device_id_type=MESH,
        )

    def along(d, step):
        shard = chip_at(step) * 2 + core
        return pltpu.make_async_remote_copy(
            src_ref=panels.at[reach, shard],
            dst_ref=panels.at[reach - d, shard],
            send_sem=along_send.at[d + reach, step],
            recv_sem=arrival.at[reach - d, shard],
            device_id={"blk": position + d},
            device_id_type=MESH,
        )

    def along_live(d):
        return pltpu.make_async_remote_copy(
            src_ref=live_ref,
            dst_ref=lives.at[reach - d],
            send_sem=live_send.at[d + reach],
            recv_sem=live_arrival.at[reach - d],
            device_id={"blk": position + d},
            device_id_type=MESH,
        )

    def arrived(d, shard):
        pltpu.make_async_copy(
            panels.at[d + reach, shard], panels.at[d + reach, shard], arrival.at[d + reach, shard]
        ).wait()

    for step in range(1, chip_count):
        across(step).start()
    for d in distances:

        @pl.when(inside(d))
        def _():
            along(d, 0).start()
            along_live(d).start()

    to_partner(0, 0).start()

    own_row = lax.broadcasted_iota(jnp.int32, (PANEL, PANEL), 0)
    own_column = lax.broadcasted_iota(jnp.int32, (PANEL, PANEL), 1)
    live_column = jnp.sum(
        jnp.where(own_row == own_column, live_row, 0.0), axis=1, keepdims=True
    )
    sums[...] = jnp.zeros_like(sums)

    for step in range(1, chip_count):
        arrived(0, chip_at(step) * 2 + core)
        to_partner(0, step).start()
        for d in distances:

            @pl.when(inside(d))
            def _():
                along(d, step).start()

    for d in distances:

        @pl.when(inside(d))
        def _():
            arrived(d, me)
            to_partner(d, 0).start()

    for step in range(chip_count):
        arrived(0, chip_at(step) * 2 + 1 - core)

    first_lag = me * lag_count
    own = panels[reach].reshape(PANEL, time_length).astype(jnp.float32)
    chunks = [own[:, i : i + LANES] for i in range(0, time_length, LANES)]
    chunks = shift_right(chunks, first_lag)
    for lag in range(lag_count):
        if lag:
            chunks = shift_right(chunks, 1)
        lagged[lag] = jnp.concatenate(chunks, axis=1).astype(jnp.bfloat16)

    def correlate(d):
        visiting = panels[d + reach].reshape(PANEL, time_length)
        rows = []
        for lag in range(lag_count):
            correlation = lax.dot_general(
                lagged[lag],
                visiting,
                (((1,), (1,)), ((), ())),
                preferred_element_type=jnp.float32,
            )
            rows.append(diagonal_totals(correlation))
        flags = live_ref[...] if d == 0 else lives[d + reach]
        rows.append(diagonal_totals(live_column * flags.astype(jnp.float32)))
        totals = jnp.concatenate(rows, axis=0)
        offset = (
            lax.broadcasted_iota(jnp.int32, totals.shape, 1) + d * PANEL - (PANEL - 1)
        )
        kept = jnp.logical_and(
            offset >= band_ref[0, 0, d + reach], offset <= band_ref[0, 1, d + reach]
        )
        kept = jnp.logical_and(kept, offset < d * PANEL + PANEL)
        start = (d + reach) * PANEL
        window = (slice(0, lag_count + 1), slice(start, start + 2 * PANEL))
        sums[window] += jnp.where(kept, totals, 0.0)

    correlate(0)

    for step in range(1, chip_count):
        for d in distances:

            @pl.when(inside(d))
            def _():
                arrived(d, chip_at(step) * 2 + core)
                to_partner(d, step).start()

    for d in distances:

        @pl.when(inside(d))
        def _():
            for step in range(chip_count):
                arrived(d, chip_at(step) * 2 + 1 - core)
            pltpu.make_async_copy(
                lives.at[d + reach], lives.at[d + reach], live_arrival.at[d + reach]
            ).wait()
            correlate(d)

    inverse = 1.0 / (jnp.maximum(sums[lag_count:], 1.0) * math.sqrt(time_length))
    out_ref[0] = sums[:lag_count] * inverse

    for step in range(1, chip_count):
        across(step).wait_send()
    for step in range(chip_count):
        to_partner(0, step).wait_send()
    for d in distances:

        @pl.when(inside(d))
        def _():
            along_live(d).wait_send()
            for step in range(chip_count):
                along(d, step).wait_send()
                to_partner(d, step).wait_send()


def on_device(strain, fir_taps, live_mask, offset_band):
    channels, raw_length = strain.shape
    time_length = raw_length // DEC
    panel_count = lax.axis_size("blk")
    sub_count = lax.axis_size("sub")
    reach = max(1, panel_count // 8)
    slots = 2 * reach + 1
    chip_count = sub_count // 2
    lag_count = LAGS // sub_count
    width = (2 * reach + 2) * PANEL
    vmem = pl.BlockSpec(memory_space=pltpu.VMEM)
    dma = pltpu.SemaphoreType.DMA
    return pl.pallas_call(
        functools.partial(kernel, panel_count, sub_count, reach),
        out_shape=jax.ShapeDtypeStruct((1, lag_count, width), jnp.float32),
        in_specs=[vmem, vmem, vmem, pl.BlockSpec(memory_space=pltpu.SMEM)],
        out_specs=vmem,
        scratch_shapes=[
            pltpu.VMEM((slots, sub_count, channels, time_length), jnp.bfloat16),
            pltpu.VMEM((slots, 1, PANEL), jnp.int32),
            pltpu.VMEM((lag_count, PANEL, time_length), jnp.bfloat16),
            pltpu.VMEM((lag_count + 1, width), jnp.float32),
            dma((chip_count,)),
            dma((slots, chip_count)),
            dma((slots, chip_count)),
            dma((slots,)),
            dma((slots, sub_count)),
            dma((slots,)),
        ],
        compiler_params=pltpu.CompilerParams(collective_id=0, has_side_effects=True),
    )(
        strain,
        fir_taps,
        live_mask.reshape(1, PANEL),
        jnp.swapaxes(offset_band, 1, 2),
    )


def solution(mesh):
    in_specs = (
        P(("groups", "blk", "sub"), None),
        P(),
        P(("groups", "blk")),
        P(("groups", "blk"), None, None),
    )
    out_specs = P(("groups", "blk"), "sub", None)
    return jax.shard_map(
        on_device, mesh=mesh, in_specs=in_specs, out_specs=out_specs, check_vma=False
    )
```

```python
import functools
import math

import jax
import jax.numpy as jnp
from jax import lax
from jax.experimental import pallas as pl
from jax.experimental.pallas import tpu as pltpu
from jax.sharding import PartitionSpec as P

PANEL = 512
DEC = 4
TAPS = 128
LAGS = 16
LANES = 128
CHUNKS = 2
MESH = pl.DeviceIdType.MESH


def shift_right(chunks, amount):
    lane = lax.broadcasted_iota(jnp.int32, chunks[0].shape, 1)
    rolled = [pltpu.roll(chunk, amount, 1) for chunk in chunks]
    before = [jnp.zeros_like(chunks[0])] + rolled[:-1]
    return [jnp.where(lane < amount, b, r) for b, r in zip(before, rolled)]


def diagonal_totals(matrix):
    blocks = PANEL // LANES
    chunks = []
    for j in range(1 - blocks, blocks):
        total = None
        for row in range(max(0, -j), min(blocks, blocks - j)):
            piece = matrix[
                row * LANES : (row + 1) * LANES, (row + j) * LANES : (row + j + 1) * LANES
            ]
            total = piece if total is None else total + piece
        chunks.append(total)
    chunks.append(jnp.zeros_like(chunks[0]))
    half = LANES // 2
    while half >= 8:
        low = shift_right([chunk[:half] for chunk in chunks], half)
        chunks = [a + b[half : 2 * half] for a, b in zip(low, chunks)]
        half //= 2
    row = lax.broadcasted_iota(jnp.int32, chunks[0].shape, 0)
    for bit in (4, 2, 1):
        moved = shift_right(chunks, bit)
        chunks = [jnp.where((row & bit) == 0, m, c) for m, c in zip(moved, chunks)]
    return jnp.concatenate([jnp.sum(c, axis=0, keepdims=True) for c in chunks], axis=1)


def filtered_normalized(strain_ref, taps_ref, own_live):
    channels, raw_length = strain_ref.shape
    time_length = raw_length // DEC
    span = LANES * DEC
    taps = jnp.concatenate([taps_ref[...].astype(jnp.float32).reshape(1, TAPS), jnp.zeros((1, span), jnp.float32)], axis=1)
    bank = jnp.broadcast_to(taps, (LANES, span + TAPS))
    bank = pltpu.roll(bank, DEC, 1, stride=DEC, stride_axis=0).astype(jnp.bfloat16)
    pieces = []
    for block in range(time_length // LANES):
        if block == 0:
            window = jnp.concatenate(
                [jnp.zeros((channels, TAPS), jnp.bfloat16), strain_ref[:, :span]], axis=1
            )
        else:
            window = strain_ref[:, block * span - TAPS : (block + 1) * span]
        pieces.append(
            lax.dot_general(
                window, bank, (((1,), (1,)), ((), ())), preferred_element_type=jnp.float32
            )
        )
    filtered = jnp.concatenate(pieces, axis=1)
    mean_square = jnp.mean(filtered * filtered, axis=1, keepdims=True)
    return (own_live * (filtered / jnp.sqrt(mean_square + 1e-6))).astype(jnp.bfloat16)


def kernel(
    panel_count,
    sub_count,
    reach,
    strain_hbm,
    taps_ref,
    live_ref,
    band_ref,
    out_ref,
    strain_ref,
    fetched,
    panels,
    lives,
    lagged,
    sums,
    across_send,
    partner_send,
    along_send,
    live_send,
    arrival,
    live_arrival,
):
    channels = strain_ref.shape[0]
    time_length = strain_ref.shape[1] // DEC
    chip_count = sub_count // 2
    lag_count = LAGS // sub_count
    position = lax.axis_index("blk")
    me = lax.axis_index("sub")
    core = lax.rem(me, 2)
    chip = lax.div(me, 2)
    partner = chip * 2 + 1 - core
    distances = [d for step in range(1, reach + 1) for d in (-step, step)]

    def inside(d):
        return jnp.logical_and(position + d >= 0, position + d < panel_count)

    def chip_at(step):
        return lax.rem(chip + step, chip_count)

    fetch = pltpu.make_async_copy(strain_hbm, strain_ref, fetched)
    fetch.start()
    barrier = pltpu.get_barrier_semaphore()
    pl.semaphore_signal(barrier, inc=1, device_id={"sub": partner}, device_id_type=MESH)
    for step in range(1, chip_count):
        pl.semaphore_signal(
            barrier, inc=1, device_id={"sub": chip_at(step) * 2 + core}, device_id_type=MESH
        )
    for d in distances:

        @pl.when(inside(d))
        def _():
            pl.semaphore_signal(
                barrier, inc=1, device_id={"blk": position + d}, device_id_type=MESH
            )

    fetch.wait()
    row = lax.broadcasted_iota(jnp.int32, (channels, PANEL), 0)
    column = lax.broadcasted_iota(jnp.int32, (channels, PANEL), 1)
    live_row = live_ref[...].astype(jnp.float32)
    own_live = jnp.sum(
        jnp.where(column == row + me * channels, live_row, 0.0), axis=1, keepdims=True
    )
    panels[reach, me] = filtered_normalized(strain_ref, taps_ref, own_live)

    pl.semaphore_wait(
        barrier,
        chip_count
        + jnp.minimum(position, reach)
        + jnp.minimum(panel_count - 1 - position, reach),
    )

    rows = channels // CHUNKS

    def shard_at(step):
        return chip_at(step) * 2 + core

    def other_at(step):
        return chip_at(step) * 2 + 1 - core

    def part(slot, shard, chunk):
        return panels.at[slot, shard, pl.ds(chunk * rows, rows)]

    def across(d, step, chunk):
        return pltpu.make_async_remote_copy(
            src_ref=part(d + reach, me, chunk),
            dst_ref=part(d + reach, me, chunk),
            send_sem=across_send.at[d + reach, step, chunk],
            recv_sem=arrival.at[d + reach, me, chunk],
            device_id={"sub": shard_at(step)},
            device_id_type=MESH,
        )

    def to_partner(d, step, chunk):
        shard = shard_at(step)
        return pltpu.make_async_remote_copy(
            src_ref=part(d + reach, shard, chunk),
            dst_ref=part(d + reach, shard, chunk),
            send_sem=partner_send.at[d + reach, step, chunk],
            recv_sem=arrival.at[d + reach, shard, chunk],
            device_id={"sub": partner},
            device_id_type=MESH,
        )

    def along(d, step, chunk):
        shard = shard_at(step)
        return pltpu.make_async_remote_copy(
            src_ref=part(reach, shard, chunk),
            dst_ref=part(reach - d, shard, chunk),
            send_sem=along_send.at[d + reach, step, chunk],
            recv_sem=arrival.at[reach - d, shard, chunk],
            device_id={"blk": position + d},
            device_id_type=MESH,
        )

    def along_live(d):
        return pltpu.make_async_remote_copy(
            src_ref=live_ref,
            dst_ref=lives.at[reach - d],
            send_sem=live_send.at[d + reach],
            recv_sem=live_arrival.at[reach - d],
            device_id={"blk": position + d},
            device_id_type=MESH,
        )

    def arrived(d, shard, chunk):
        view = part(d + reach, shard, chunk)
        pltpu.make_async_copy(view, view, arrival.at[d + reach, shard, chunk]).wait()

    for chunk in range(CHUNKS):
        for step in range(1, chip_count):
            across(0, step, chunk).start()
    for d in distances:

        @pl.when(inside(d))
        def _():
            for chunk in range(CHUNKS):
                along(d, 0, chunk).start()
            along_live(d).start()
    for chunk in range(CHUNKS):
        to_partner(0, 0, chunk).start()

    own_row = lax.broadcasted_iota(jnp.int32, (PANEL, PANEL), 0)
    own_column = lax.broadcasted_iota(jnp.int32, (PANEL, PANEL), 1)
    live_column = jnp.sum(
        jnp.where(own_row == own_column, live_row, 0.0), axis=1, keepdims=True
    )
    sums[...] = jnp.zeros_like(sums)

    first_lag = me * lag_count

    def delay_chip(step):
        visitor = chip_at(step)
        own = panels[reach, pl.ds(visitor * 2, 2)].reshape(2 * channels, time_length)
        own = own.astype(jnp.float32)
        chunks = [own[:, i : i + LANES] for i in range(0, time_length, LANES)]
        chunks = shift_right(chunks, first_lag)
        target = pl.ds(pl.multiple_of(visitor * 2 * channels, 2 * channels), 2 * channels)
        for lag in range(lag_count):
            if lag:
                chunks = shift_right(chunks, 1)
            lagged[lag, target] = jnp.concatenate(chunks, axis=1).astype(jnp.bfloat16)

    for chunk in range(CHUNKS):
        arrived(0, other_at(0), chunk)
    delay_chip(0)

    for chunk in range(CHUNKS):
        for step in range(1, chip_count):
            arrived(0, shard_at(step), chunk)
            for d in distances:

                @pl.when(inside(d))
                def _():
                    along(d, step, chunk).start()

            to_partner(0, step, chunk).start()
    for d in distances:

        @pl.when(inside(d))
        def _():
            for chunk in range(CHUNKS):
                arrived(d, me, chunk)
                to_partner(d, 0, chunk).start()

    for step in range(1, chip_count):
        for chunk in range(CHUNKS):
            arrived(0, other_at(step), chunk)
        delay_chip(step)

    def totals_of(d):
        visiting = panels[d + reach].reshape(PANEL, time_length)
        rows = []
        for lag in range(lag_count):
            correlation = lax.dot_general(
                lagged[lag],
                visiting,
                (((1,), (1,)), ((), ())),
                preferred_element_type=jnp.float32,
            )
            rows.append(diagonal_totals(correlation))
        flags = live_ref[...] if d == 0 else lives[d + reach]
        rows.append(diagonal_totals(live_column * flags.astype(jnp.float32)))
        return jnp.concatenate(rows, axis=0)

    def accumulate(d, totals):
        offset = (
            lax.broadcasted_iota(jnp.int32, totals.shape, 1) + d * PANEL - (PANEL - 1)
        )
        kept = jnp.logical_and(
            offset >= band_ref[0, 0, d + reach], offset <= band_ref[0, 1, d + reach]
        )
        kept = jnp.logical_and(kept, offset < d * PANEL + PANEL)
        start = (d + reach) * PANEL
        window = (slice(0, lag_count + 1), slice(start, start + 2 * PANEL))
        sums[window] += jnp.where(kept, totals, 0.0)

    accumulate(0, totals_of(0))

    for chunk in range(CHUNKS):
        for d in distances:

            @pl.when(inside(d))
            def _():
                for step in range(1, chip_count):
                    arrived(d, shard_at(step), chunk)
                    to_partner(d, step, chunk).start()

    def settle(d):
        for step in range(chip_count):
            for chunk in range(CHUNKS):
                arrived(d, other_at(step), chunk)
        pltpu.make_async_copy(
            lives.at[d + reach], lives.at[d + reach], live_arrival.at[d + reach]
        ).wait()

    for near in range(0, len(distances), 2):
        pair = distances[near : near + 2]
        both = jnp.logical_and(inside(pair[0]), inside(pair[1]))

        @pl.when(both)
        def _():
            for d in pair:
                settle(d)
            found = [totals_of(d) for d in pair]
            for d, totals in zip(pair, found):
                accumulate(d, totals)

        for d in pair:

            @pl.when(jnp.logical_and(inside(d), jnp.logical_not(both)))
            def _():
                settle(d)
                accumulate(d, totals_of(d))

    inverse = 1.0 / (jnp.maximum(sums[lag_count:], 1.0) * math.sqrt(time_length))
    out_ref[0] = sums[:lag_count] * inverse

    for chunk in range(CHUNKS):
        for step in range(1, chip_count):
            across(0, step, chunk).wait_send()
        for step in range(chip_count):
            to_partner(0, step, chunk).wait_send()
    for d in distances:

        @pl.when(inside(d))
        def _():
            along_live(d).wait_send()
            for chunk in range(CHUNKS):
                along(d, 0, chunk).wait_send()
                for step in range(1, chip_count):
                    along(d, step, chunk).wait_send()
                for step in range(chip_count):
                    to_partner(d, step, chunk).wait_send()


def on_device(strain, fir_taps, live_mask, offset_band):
    channels, raw_length = strain.shape
    time_length = raw_length // DEC
    panel_count = lax.axis_size("blk")
    sub_count = lax.axis_size("sub")
    reach = max(1, panel_count // 8)
    slots = 2 * reach + 1
    chip_count = sub_count // 2
    lag_count = LAGS // sub_count
    width = (2 * reach + 2) * PANEL
    vmem = pl.BlockSpec(memory_space=pltpu.VMEM)
    dma = pltpu.SemaphoreType.DMA
    return pl.pallas_call(
        functools.partial(kernel, panel_count, sub_count, reach),
        out_shape=jax.ShapeDtypeStruct((1, lag_count, width), jnp.float32),
        in_specs=[pl.BlockSpec(memory_space=pl.ANY), vmem, vmem, pl.BlockSpec(memory_space=pltpu.SMEM)],
        out_specs=vmem,
        scratch_shapes=[
            pltpu.VMEM((channels, raw_length), jnp.bfloat16),
            dma,
            pltpu.VMEM((slots, sub_count, channels, time_length), jnp.bfloat16),
            pltpu.VMEM((slots, 1, PANEL), jnp.int32),
            pltpu.VMEM((lag_count, PANEL, time_length), jnp.bfloat16),
            pltpu.VMEM((lag_count + 1, width), jnp.float32),
            dma((slots, chip_count, CHUNKS)),
            dma((slots, chip_count, CHUNKS)),
            dma((slots, chip_count, CHUNKS)),
            dma((slots,)),
            dma((slots, sub_count, CHUNKS)),
            dma((slots,)),
        ],
        compiler_params=pltpu.CompilerParams(
            collective_id=0, has_side_effects=True, vmem_limit_bytes=24 << 20
        ),
    )(
        strain,
        fir_taps,
        live_mask.reshape(1, PANEL),
        jnp.swapaxes(offset_band, 1, 2),
    )


def solution(mesh):
    in_specs = (
        P(("groups", "blk", "sub"), None),
        P(),
        P(("groups", "blk")),
        P(("groups", "blk"), None, None),
    )
    out_specs = P(("groups", "blk"), "sub", None)
    return jax.shard_map(
        on_device, mesh=mesh, in_specs=in_specs, out_specs=out_specs, check_vma=False
    )
```
